32 devices in a mesh: dp: 2 (over x), segment: 4 (over y, core), space: 4 (over z).
Axes of the slice: x: 2, y: 2, z: 4, core: 2. Of those that a mesh axis runs over, the one named last changes fastest.
Arguments:
- features: bfloat16 [2, 4, 32, 24, 6, 256], P('dp', 'segment', None, 'space'), may hold values from -6 to 6
- out_grad: bfloat16 [2, 4, 64, 12, 3, 128], P('dp', 'segment', None, 'space'), may hold values from -6 to 6
- weight_mean: float32 [4, 27, 2048], P('segment'), may hold values from -0.21875 to 0.21875
- weight_noise: float32 [4, 27, 2048], P('segment'), may hold values from -4 to 4
- precision: float32 [4, 27, 2048], P('segment'), may hold values from 0.5 to 4
Outputs:
- act_in: bfloat16 [2, 4, 64, 12, 3, 128], P('dp', 'segment', None, 'space')
- grad_in: bfloat16 [2, 4, 32, 24, 6, 256], P('dp', 'segment', None, 'space')
- mean_next: float32 [4, 27, 2048], P('segment')
- precision_next: float32 [4, 27, 2048], P('segment')
The draws below stay inside these ranges and needn't reach their ends.
All inputs are finite; a program needn't handle non-finite values.
Results may differ from the reference program's by a relative error of at most 0.007.
Values may be sent and summed in bfloat16 or wider, within the bound.
No kernel may reach another device: no remote copies, remote signals or barrier semaphores. Data moves between devices by JAX's collectives and lax.ppermute only.
A program may use at most 64 MiB of HBM per device.

```python
import math
import jax
import jax.numpy as jnp
from jax import lax

CIN = 32
COUT = 64
XD = 6
YS = 6
ZS = 256
N_DP = 2
N_SEGMENT = 4
N_SPACE = 4


def level_of(stream_key, shape, shards, low, largest):
    gain, own = 1.0, jax.random.fold_in(stream_key, 6)
    for dim, shards_of in shards:
        steps = jnp.exp(jax.random.uniform(jax.random.fold_in(own, dim), (shards_of,), jnp.float32, low / len(shards), largest / len(shards)))
        gain = gain * jnp.repeat(steps, shape[dim] // shards_of).reshape([-1 if axis == dim else 1 for axis in range(len(shape))])
    return gain


def normal_values(key, extent, width, reach, split=(), dtype=jnp.bfloat16):
    loudness = level_of(key, extent, split, -0.22, 0.18) if split else 1.0
    values = jax.random.normal(key, extent, jnp.float32) * width * loudness
    return jnp.minimum(jnp.maximum(values, -reach), reach).astype(dtype)


def setup_inputs(seed: int = 0) -> dict:
    splits = jax.random.split(jax.random.key(seed), 6)
    return {
        "features": normal_values(splits[0], (N_DP, N_SEGMENT, CIN, XD * N_SPACE, YS, ZS), 1.0, 6.0, ((0, 2), (1, 4), (3, 4))),
        "out_grad": normal_values(splits[1], (N_DP, N_SEGMENT, COUT, XD // 2 * N_SPACE, YS // 2, ZS // 2), 1.0, 6.0, ((0, 2), (1, 4), (3, 4))),
        "weight_mean": normal_values(splits[2], (N_SEGMENT, 27, COUT * CIN), (27 * CIN) ** -0.5, 0.21875, ((0, 4),), jnp.float32),
        "weight_noise": normal_values(splits[3], (N_SEGMENT, 27, COUT * CIN), 1.0, 4.0, ((0, 4),), jnp.float32),
        "precision": jnp.clip(jnp.exp(math.log(4.0) - 2.0794415 * jax.random.uniform(splits[4], (N_SEGMENT, 27, COUT * CIN), jnp.float32) ** level_of(splits[4], (N_SEGMENT, 27, COUT * CIN), ((0, 4),), -0.2, 0.2)), 0.5, 4.0),
    }


CONV_LAYOUT = ('NCDHW', 'OIDHW', 'NCDHW')

def noisy_weights(weight_mean, weight_noise, precision, cout, cin):
    noisy = weight_mean + weight_noise * lax.rsqrt(2000.0 * (precision + 0.1))
    kernel = noisy.astype(jnp.bfloat16).reshape(3, 3, 3, cout, cin)
    return jnp.transpose(kernel, (3, 4, 0, 1, 2))

def forward_conv(padded, kernel):
    return lax.conv_general_dilated(padded[None], kernel, (2, 2, 2), 'VALID', dimension_numbers=CONV_LAYOUT, preferred_element_type=jnp.float32)[0]

def input_conv(pre_grad, kernel):
    flipped = jnp.transpose(kernel[:, :, ::-1, ::-1, ::-1], (1, 0, 2, 3, 4))
    return lax.conv_general_dilated(pre_grad[None], flipped, (1, 1, 1), ((2, 2), (2, 2), (2, 2)), lhs_dilation=(2, 2, 2), dimension_numbers=CONV_LAYOUT, preferred_element_type=jnp.float32)[0]

def weight_conv(padded, pre_grad):
    grads = lax.conv_general_dilated(padded[:, None], pre_grad[:, None], (1, 1, 1), 'VALID', rhs_dilation=(2, 2, 2), dimension_numbers=CONV_LAYOUT, preferred_element_type=jnp.float32)
    return jnp.transpose(grads, (2, 3, 4, 1, 0)).reshape(27, -1)

def reference(features, out_grad, weight_mean, weight_noise, precision):
    cell_count = N_DP * N_SPACE * (XD // 2) * (YS // 2) * (ZS // 2)
    inv_root = 1.0 / math.sqrt(cell_count)

    def per_segment(segment_item):
        feats, grads, mean, noise, prec = segment_item
        kernel = noisy_weights(mean, noise, prec, COUT, CIN)
        outputs = []
        input_grads = []
        grad_total = jnp.zeros((27, COUT * CIN), jnp.float32)
        for replica in range(N_DP):
            padded = jnp.pad(feats[replica], ((0, 0), (1, 0), (1, 0), (1, 0)))
            preact = forward_conv(padded, kernel)
            outputs.append(jax.nn.silu(preact).astype(jnp.bfloat16))
            squash = jax.nn.sigmoid(preact)
            pre_grad = (grads[replica].astype(jnp.float32) * squash * (1.0 + preact * (1.0 - squash))).astype(jnp.bfloat16)
            spread_grad = input_conv(pre_grad, kernel)
            input_grads.append(spread_grad[:, 1:, 1:, 1:])
            grad_total = grad_total + weight_conv(padded, pre_grad)
        scaled = grad_total * inv_root
        prec_next = 0.75 * prec + 0.25 * scaled * scaled
        mean_new = mean - 0.03 * scaled / (prec_next + 0.1)
        return (jnp.stack(outputs), jnp.stack(input_grads).astype(jnp.bfloat16), mean_new, prec_next)
    outputs, input_grads, mean_next, precision_next = lax.map(per_segment, (jnp.swapaxes(features, 0, 1), jnp.swapaxes(out_grad, 0, 1), weight_mean, weight_noise, precision))
    outputs = jnp.swapaxes(outputs, 0, 1)
    input_grads = jnp.swapaxes(input_grads, 0, 1)
    act_in = jnp.concatenate([jnp.zeros_like(outputs[:, :1]), outputs[:, :-1]], axis=1)
    grad_in = jnp.concatenate([input_grads[:, 1:], jnp.zeros_like(input_grads[:, :1])], axis=1)
    return (act_in, grad_in, mean_next, precision_next)
```

```python
import functools
import math

import jax
import jax.numpy as jnp
from jax import lax
from jax.experimental import pallas as pl
from jax.experimental.pallas import tpu as pltpu
from jax.sharding import PartitionSpec as P

LANES = 128
TAPS = tuple((a, b, e) for a in range(3) for b in range(3) for e in range(3))
F32 = jnp.float32
BF16 = jnp.bfloat16


def passed_along(block, axis, distance):
    devices = range(lax.axis_size(axis))
    route = [(i - distance, i) for i in devices if i - distance in devices]
    return lax.ppermute(block, axis, route)


def matmul(a, b):
    return jnp.dot(a, b, preferred_element_type=F32)


def matmul_nt(a, b):
    return lax.dot_general(a, b, (((1,), (1,)), ((), ())), preferred_element_type=F32)


def iota(shape, dim):
    return lax.broadcasted_iota(jnp.int32, shape, dim)


def as_bf16(mask):
    return jnp.where(mask, 1.0, 0.0).astype(BF16)


def pick_strided(zs):
    half = zs // 2
    z = iota((zs, 3 * half), 0)
    n = iota((zs, 3 * half), 1)
    e = jnp.where(n >= 2 * half, 2, jnp.where(n >= half, 1, 0))
    return as_bf16(z == 2 * (n - e * half) + e - 1)


def spread_strided(zs):
    half = zs // 2
    row = iota((zs, zs), 0)
    z = iota((zs, zs), 1)
    p = jnp.where(row >= half, 1, 0)
    return as_bf16(z == 2 * (row - p * half) + p)


def regroup(cout, groups):
    per = cout // groups
    o = iota((cout, cout), 0)
    m = iota((cout, cout), 1)
    oi = jnp.zeros_like(m)
    for step in range(1, groups):
        oi = oi + jnp.where(m >= step * per, 1, 0)
    return as_bf16(o == (m - oi * per) * groups + oi)


def weight_matrix(noisy, cout, cin):
    groups = LANES // cin
    rows = cout // groups
    lane = iota((rows, LANES), 1)
    blocks = []
    for first in range(0, len(TAPS), groups):
        parts = []
        for oi in range(groups):
            part = jnp.zeros((rows, LANES), F32)
            for t in range(groups):
                if first + t >= len(TAPS):
                    continue
                tap = noisy[(first + t) * rows : (first + t + 1) * rows]
                shift = (t - oi) * cin % LANES
                tap = pltpu.roll(tap, shift, 1) if shift else tap
                keep = (lane >= t * cin) & (lane < (t + 1) * cin)
                part = jnp.where(keep, tap, part)
            parts.append(part)
        blocks.append(jnp.concatenate(parts, axis=0))
    mixed = jnp.concatenate(blocks, axis=1).astype(BF16)
    return matmul(regroup(cout, groups), mixed).astype(BF16)


def weight_rows(total, cout, cin):
    groups = LANES // cin
    rows = cout // groups
    lane = iota((rows, LANES), 1)
    mixed = lax.dot_general(
        regroup(cout, groups),
        total.astype(BF16),
        (((0,), (0,)), ((), ())),
        preferred_element_type=F32,
    )
    out = []
    for tap in range(len(TAPS)):
        t = tap % groups
        start = (tap // groups) * LANES
        row = jnp.zeros((rows, LANES), F32)
        for oi in range(groups):
            part = mixed[oi * rows : (oi + 1) * rows, start : start + LANES]
            shift = (oi - t) * cin % LANES
            part = pltpu.roll(part, shift, 1) if shift else part
            keep = (lane >= oi * cin) & (lane < (oi + 1) * cin)
            row = jnp.where(keep, part, row)
        out.append(row)
    return jnp.concatenate(out, axis=0).astype(BF16)


def forward_kernel(x_ref, halo_ref, g_ref, mean_ref, noise_ref, prec_ref,
                   act_ref, pre_ref, w_ref, dw_ref, col_ref):
    xd, ys, cin, zs = x_ref.shape
    ni, nj, cout, half = g_ref.shape
    width = w_ref.shape[1]
    noisy = mean_ref[...] + noise_ref[...] * lax.rsqrt(2000.0 * (prec_ref[...] + 0.1))
    weights = weight_matrix(noisy, cout, cin)
    w_ref[...] = weights
    pick = pick_strided(zs)
    col_ref[:, len(TAPS) * cin :, :] = jnp.zeros((ni, width - len(TAPS) * cin, nj * half), BF16)
    for x in range(-1, xd):
        plane = halo_ref[...] if x < 0 else x_ref[x]
        picked = matmul(plane.reshape(ys * cin, zs), pick).astype(BF16)
        for tap, (a, b, e) in enumerate(TAPS):
            i = (x + 1 - a) // 2
            if 2 * i + a - 1 != x or not 0 <= i < ni:
                continue
            for j in range(nj):
                y = 2 * j + b - 1
                if y < 0:
                    block = jnp.zeros((cin, half), BF16)
                else:
                    block = picked[y * cin : (y + 1) * cin, e * half : (e + 1) * half]
                col_ref[i, tap * cin : (tap + 1) * cin, j * half : (j + 1) * half] = block
    total = jnp.zeros((cout, width), F32)
    for i in range(ni):
        preact = matmul(weights, col_ref[i])
        squash = jax.nn.sigmoid(preact)
        act = (preact * squash).astype(BF16)
        for j in range(nj):
            act_ref[i, j] = act[:, j * half : (j + 1) * half]
        grads = jnp.concatenate([g_ref[i, j] for j in range(nj)], axis=1).astype(F32)
        pre = (grads * squash * (1.0 + preact * (1.0 - squash))).astype(BF16)
        pre_ref[i] = pre
        total = total + matmul_nt(pre, col_ref[i])
    dw_ref[...] = weight_rows(total, cout, cin)


def parity_taps(parity, shift):
    if parity == 0:
        return 1 if shift == 0 else None
    return 2 if shift == 0 else 0


def input_kernel(pre_ref, rim_ref, w_ref, out_ref, wt_ref, col_ref):
    xd, ys, cin, zs = out_ref.shape
    ni, cout, _ = pre_ref.shape
    half = zs // 2
    nj = ys // 2
    combos = [(p, q, r) for p in range(2) for q in range(2) for r in range(2)]
    flipped = jnp.transpose(
        jnp.concatenate([w_ref[...].astype(F32), jnp.zeros((LANES - cout, w_ref.shape[1]), F32)], axis=0)
    )
    for row, (px, py, pz) in enumerate(combos):
        for col, (di, dj) in enumerate((u, v) for u in range(2) for v in range(2)):
            pair = jnp.zeros((cin, LANES), F32)
            for dk in range(2):
                found = (parity_taps(px, di), parity_taps(py, dj), parity_taps(pz, dk))
                if None in found:
                    continue
                tap = TAPS.index(found)
                block = flipped[tap * cin : (tap + 1) * cin]
                pair = pair + (pltpu.roll(block, cout, 1) if dk else block)
            wt_ref[row * cin : (row + 1) * cin, col * LANES : (col + 1) * LANES] = pair.astype(BF16)
    last = iota((cout, half), 1) == half - 1
    for i in range(ni + 1):
        for j in range(nj + 1):
            if j == nj:
                here = jnp.zeros((cout, half), BF16)
                ahead = here
            else:
                source = rim_ref[...] if i == ni else pre_ref[i]
                here = source[:, j * half : (j + 1) * half]
                ahead = pltpu.roll(here.astype(F32), half - 1, 1)
                ahead = jnp.where(last, 0.0, ahead).astype(BF16)
            for di in range(2):
                for dj in range(2):
                    if not (0 <= i - di < ni and 0 <= j - dj < nj):
                        continue
                    row = (2 * di + dj) * 2 * cout
                    lane = ((i - di) * nj + j - dj) * half
                    col_ref[row : row + cout, lane : lane + half] = here
                    col_ref[row + cout : row + 2 * cout, lane : lane + half] = ahead
    spread = spread_strided(zs)
    for i in range(ni):
        for j in range(nj):
            lane = (i * nj + j) * half
            cells = matmul(wt_ref[...], col_ref[:, lane : lane + half]).astype(BF16)
            pairs = jnp.concatenate(
                [
                    jnp.concatenate(
                        [cells[(2 * n) * cin : (2 * n + 1) * cin], cells[(2 * n + 1) * cin : (2 * n + 2) * cin]],
                        axis=1,
                    )
                    for n in range(4)
                ],
                axis=0,
            )
            planes = matmul(pairs, spread).astype(BF16)
            for n in range(4):
                out_ref[2 * i + n // 2, 2 * j + n % 2] = planes[n * cin : (n + 1) * cin]


def add_up(block, axis):
    size = lax.axis_size(axis)
    if size & (size - 1):
        return lax.psum(block, axis)
    step = 1
    while step < size:
        other = lax.ppermute(block, axis, [(i, i ^ step) for i in range(size)])
        block = (block.astype(F32) + other.astype(F32)).astype(BF16)
        step *= 2
    return block


def per_device(features, out_grad, weight_mean, weight_noise, precision):
    feats = jnp.transpose(features[0, 0], (1, 2, 0, 3))
    grads = jnp.transpose(out_grad[0, 0], (1, 2, 0, 3))
    xd, ys, cin, zs = feats.shape
    ni, nj, cout, half = grads.shape
    flat = (weight_mean.size // LANES, LANES)
    mean = weight_mean.reshape(flat)
    prec = precision.reshape(flat)
    noise = weight_noise.reshape(flat)
    width = pl.cdiv(len(TAPS) * cin, LANES) * LANES

    below = passed_along(feats[xd - 1], "space", 1)
    act, pre, weights, dw = pl.pallas_call(
        forward_kernel,
        out_shape=(
            jax.ShapeDtypeStruct((ni, nj, cout, half), BF16),
            jax.ShapeDtypeStruct((ni, cout, nj * half), BF16),
            jax.ShapeDtypeStruct((cout, width), BF16),
            jax.ShapeDtypeStruct(flat, BF16),
        ),
        scratch_shapes=[pltpu.VMEM((ni, width, nj * half), BF16)],
        name="forward",
    )(feats, below, grads, mean, noise, prec)
    rim = passed_along(pre[0], "space", -1)
    act_in = passed_along(act, "segment", 1)
    spread_grad = pl.pallas_call(
        input_kernel,
        out_shape=jax.ShapeDtypeStruct((xd, ys, cin, zs), BF16),
        scratch_shapes=[
            pltpu.VMEM((8 * cin, 8 * cout), BF16),
            pltpu.VMEM((8 * cout, ni * nj * half), BF16),
        ],
        name="input_grad",
    )(pre, rim, weights)
    grad_in = passed_along(spread_grad, "segment", -1)

    cell_count = lax.axis_size("dp") * lax.axis_size("space") * ni * nj * half
    inv_root = 1.0 / math.sqrt(cell_count)
    grad_total = add_up(add_up(dw, "dp"), "space").astype(F32)
    scaled = grad_total * inv_root
    prec_next = 0.75 * prec + 0.25 * scaled * scaled
    mean_next = mean - 0.03 * scaled / (prec_next + 0.1)
    return (
        jnp.transpose(act_in, (2, 0, 1, 3))[None, None],
        jnp.transpose(grad_in, (2, 0, 1, 3))[None, None],
        mean_next.reshape(weight_mean.shape),
        prec_next.reshape(precision.shape),
    )


def solution(mesh):
    in_specs = (
        P("dp", "segment", None, "space", None, None),
        P("dp", "segment", None, "space", None, None),
        P("segment", None, None),
        P("segment", None, None),
        P("segment", None, None),
    )
    out_specs = (
        P("dp", "segment", None, "space", None, None),
        P("dp", "segment", None, "space", None, None),
        P("segment", None, None),
        P("segment", None, None),
    )
    return jax.shard_map(
        per_device, mesh=mesh, in_specs=in_specs, out_specs=out_specs, check_vma=False
    )
```

```python
import math

import jax
import jax.numpy as jnp
from jax import lax
from jax.experimental import pallas as pl
from jax.experimental.pallas import tpu as pltpu
from jax.sharding import PartitionSpec as P


LANES = 128
TAPS = tuple((a, b, e) for a in range(3) for b in range(3) for e in range(3))
F32 = jnp.float32
BF16 = jnp.bfloat16


def passed_along(block, axis, distance):
    devices = range(lax.axis_size(axis))
    route = [(i - distance, i) for i in devices if i - distance in devices]
    return lax.ppermute(block, axis, route)


def matmul(a, b):
    return jnp.dot(a, b, preferred_element_type=F32)


def matmul_nt(a, b):
    return lax.dot_general(a, b, (((1,), (1,)), ((), ())), preferred_element_type=F32)


def passed_diagonally(block):
    n_segment, n_space = lax.axis_size("segment"), lax.axis_size("space")
    route = [
        ((s + 1) * n_space + z + 1, s * n_space + z)
        for s in range(n_segment - 1)
        for z in range(n_space - 1)
    ]
    return lax.ppermute(block, ("segment", "space"), route)


def iota(shape, dim):
    return lax.broadcasted_iota(jnp.int32, shape, dim)


def as_bf16(mask):
    return jnp.where(mask, 1.0, 0.0).astype(BF16)


def pick_strided(zs):
    half = zs // 2
    z = iota((zs, 3 * half), 0)
    n = iota((zs, 3 * half), 1)
    e = jnp.where(n >= 2 * half, 2, jnp.where(n >= half, 1, 0))
    return as_bf16(z == 2 * (n - e * half) + e - 1)


def spread_strided(zs):
    half = zs // 2
    row = iota((zs, zs), 0)
    z = iota((zs, zs), 1)
    p = jnp.where(row >= half, 1, 0)
    return as_bf16(z == 2 * (row - p * half) + p)


def regroup(cout, groups):
    per = cout // groups
    o = iota((cout, cout), 0)
    m = iota((cout, cout), 1)
    oi = jnp.zeros_like(m)
    for step in range(1, groups):
        oi = oi + jnp.where(m >= step * per, 1, 0)
    return as_bf16(o == (m - oi * per) * groups + oi)


def weight_matrix(noisy, cout, cin):
    groups = LANES // cin
    rows = cout // groups
    lane = iota((rows, LANES), 1)
    blocks = []
    for first in range(0, len(TAPS), groups):
        parts = []
        for oi in range(groups):
            part = jnp.zeros((rows, LANES), F32)
            for t in range(groups):
                if first + t >= len(TAPS):
                    continue
                tap = noisy[(first + t) * rows : (first + t + 1) * rows]
                shift = (t - oi) * cin % LANES
                tap = pltpu.roll(tap, shift, 1) if shift else tap
                keep = (lane >= t * cin) & (lane < (t + 1) * cin)
                part = jnp.where(keep, tap, part)
            parts.append(part)
        blocks.append(jnp.concatenate(parts, axis=0))
    mixed = jnp.concatenate(blocks, axis=1).astype(BF16)
    return matmul(regroup(cout, groups), mixed).astype(BF16)


def weight_rows(total, cout, cin):
    groups = LANES // cin
    rows = cout // groups
    lane = iota((rows, LANES), 1)
    mixed = lax.dot_general(
        regroup(cout, groups),
        total.astype(BF16),
        (((0,), (0,)), ((), ())),
        preferred_element_type=F32,
    )
    out = []
    for tap in range(len(TAPS)):
        t = tap % groups
        start = (tap // groups) * LANES
        row = jnp.zeros((rows, LANES), F32)
        for oi in range(groups):
            part = mixed[oi * rows : (oi + 1) * rows, start : start + LANES]
            shift = (oi - t) * cin % LANES
            part = pltpu.roll(part, shift, 1) if shift else part
            keep = (lane >= oi * cin) & (lane < (oi + 1) * cin)
            row = jnp.where(keep, part, row)
        out.append(row)
    return jnp.concatenate(out, axis=0).astype(BF16)


def activate(preact, grads):
    squash = jax.nn.sigmoid(preact)
    act = (preact * squash).astype(BF16)
    pre = (grads * squash * (1.0 + preact * (1.0 - squash))).astype(BF16)
    return act, pre


def place_plane(picked, x, ys, cin, half, targets):
    for tap, (a, b, e) in enumerate(TAPS):
        i = (x + 1 - a) // 2
        if 2 * i + a - 1 != x or i not in targets:
            continue
        for j in range(ys // 2):
            y = 2 * j + b - 1
            if y < 0:
                block = jnp.zeros((cin, half), BF16)
            else:
                block = picked[y * cin : (y + 1) * cin, e * half : (e + 1) * half]
            targets[i][tap * cin : (tap + 1) * cin, j * half : (j + 1) * half] = block


def prepare_kernel(x_hbm, g_hbm, mean_hbm, noise_hbm, prec_hbm,
                   act_ref, pre_ref, w_ref, part_ref, total_ref, col_ref,
                   x_ref, g_ref, mean_ref, noise_ref, prec_ref, cols_ref, sems):
    xd, ys, cin, zs = x_ref.shape
    ni, nj, cout, half = g_ref.shape
    width = w_ref.shape[1]
    depth = len(TAPS) * cin
    order = [pltpu.make_async_copy(x_hbm.at[x], x_ref.at[x], sems.at[x]) for x in range(xd)]
    pairs = ((mean_hbm, mean_ref), (noise_hbm, noise_ref), (prec_hbm, prec_ref), (g_hbm, g_ref))
    rest = [pltpu.make_async_copy(src, dst, sems.at[xd + n]) for n, (src, dst) in enumerate(pairs)]
    for copy in order + rest:
        copy.start()
    targets = {0: col_ref, **{i: cols_ref.at[i - 1] for i in range(1, ni)}}
    for ref in targets.values():
        ref[depth:, :] = jnp.zeros((width - depth, nj * half), BF16)
    pick = pick_strided(zs)
    for x in range(xd):
        order[x].wait()
        picked = matmul(x_ref[x].reshape(ys * cin, zs), pick).astype(BF16)
        place_plane(picked, x, ys, cin, half, targets)
    for copy in rest:
        copy.wait()
    noisy = mean_ref[...] + noise_ref[...] * lax.rsqrt(2000.0 * (prec_ref[...] + 0.1))
    weights = weight_matrix(noisy, cout, cin)
    w_ref[...] = weights
    total = jnp.zeros((cout, width), F32)
    for i in range(1, ni):
        preact = matmul(weights, cols_ref[i - 1])
        grads = jnp.concatenate([g_ref[i, j] for j in range(nj)], axis=1).astype(F32)
        act, pre = activate(preact, grads)
        for j in range(nj):
            act_ref[i - 1, j] = act[:, j * half : (j + 1) * half]
        pre_ref[i - 1] = pre
        total = total + matmul_nt(pre, cols_ref[i - 1])
    total_ref[...] = total
    first = depth // 3
    part_ref[...] = matmul(weights[:, first:], col_ref[first:, :])


def finish_kernel(halo_ref, act_rest_ref, pre_rest_ref, w_ref, part_ref, total_ref, col_in_ref, g_hbm,
                  act_ref, pack_ref, rim_ref, dw_ref, col_ref, g_ref, sem):
    ys, cin, zs = halo_ref.shape
    ni, nj, cout, half = act_ref.shape
    first = len(TAPS) * cin // 3
    copy = pltpu.make_async_copy(g_hbm.at[0], g_ref, sem)
    copy.start()
    picked = matmul(halo_ref[...].reshape(ys * cin, zs), pick_strided(zs)).astype(BF16)
    place_plane(picked, -1, ys, cin, half, {0: col_ref})
    preact = part_ref[...] + matmul(w_ref[:, :first], col_ref[...])
    copy.wait()
    grads = jnp.concatenate([g_ref[j] for j in range(nj)], axis=1).astype(F32)
    act, pre = activate(preact, grads)
    for j in range(nj):
        act_ref[0, j] = act[:, j * half : (j + 1) * half]
    act_ref[1:] = act_rest_ref[...]
    rim_ref[...] = pre
    pack_ref[:, : nj * half] = pre
    for i in range(1, ni):
        pack_ref[:, i * nj * half : (i + 1) * nj * half] = pre_rest_ref[i - 1]
    pack_ref[:, ni * nj * half :] = w_ref[...]
    ours = jnp.concatenate([matmul_nt(pre, col_ref[...]), matmul_nt(pre, col_in_ref[first:, :])], axis=1)
    dw_ref[...] = weight_rows(total_ref[...] + ours, cout, cin)


def parity_taps(parity, shift):
    if parity == 0:
        return 1 if shift == 0 else None
    return 2 if shift == 0 else 0


def input_kernel(pack_ref, rim_ref, out_ref, wt_ref, col_ref):
    xd, ys, cin, zs = out_ref.shape
    cout = pack_ref.shape[0]
    half = zs // 2
    ni, nj = xd // 2, ys // 2
    weights = pack_ref[:, ni * nj * half :]
    combos = [(p, q, r) for p in range(2) for q in range(2) for r in range(2)]
    flipped = jnp.transpose(
        jnp.concatenate([weights.astype(F32), jnp.zeros((LANES - cout, weights.shape[1]), F32)], axis=0)
    )
    for row, (px, py, pz) in enumerate(combos):
        for col, (di, dj) in enumerate((u, v) for u in range(2) for v in range(2)):
            pair = jnp.zeros((cin, LANES), F32)
            for dk in range(2):
                found = (parity_taps(px, di), parity_taps(py, dj), parity_taps(pz, dk))
                if None in found:
                    continue
                tap = TAPS.index(found)
                block = flipped[tap * cin : (tap + 1) * cin]
                pair = pair + (pltpu.roll(block, cout, 1) if dk else block)
            wt_ref[row * cin : (row + 1) * cin, col * LANES : (col + 1) * LANES] = pair.astype(BF16)
    last = iota((cout, half), 1) == half - 1
    for i in range(ni + 1):
        for j in range(nj + 1):
            if j == nj:
                here = jnp.zeros((cout, half), BF16)
                ahead = here
            else:
                lane = (i * nj + j) * half
                here = rim_ref[:, j * half : (j + 1) * half] if i == ni else pack_ref[:, lane : lane + half]
                ahead = pltpu.roll(here.astype(F32), half - 1, 1)
                ahead = jnp.where(last, 0.0, ahead).astype(BF16)
            for di in range(2):
                for dj in range(2):
                    if not (0 <= i - di < ni and 0 <= j - dj < nj):
                        continue
                    row = (2 * di + dj) * 2 * cout
                    lane = ((i - di) * nj + j - dj) * half
                    col_ref[row : row + cout, lane : lane + half] = here
                    col_ref[row + cout : row + 2 * cout, lane : lane + half] = ahead
    spread = spread_strided(zs)
    for i in range(ni):
        for j in range(nj):
            lane = (i * nj + j) * half
            cells = matmul(wt_ref[...], col_ref[:, lane : lane + half]).astype(BF16)
            pairs = jnp.concatenate(
                [
                    jnp.concatenate(
                        [cells[(2 * n) * cin : (2 * n + 1) * cin], cells[(2 * n + 1) * cin : (2 * n + 2) * cin]],
                        axis=1,
                    )
                    for n in range(4)
                ],
                axis=0,
            )
            planes = matmul(pairs, spread).astype(BF16)
            for n in range(4):
                out_ref[2 * i + n // 2, 2 * j + n % 2] = planes[n * cin : (n + 1) * cin]


def copy_kernel(src_ref, out_ref):
    out_ref[...] = src_ref[...]


def swapped(block, flip_dp, flip_space):
    n_space = lax.axis_size("space")
    route = [
        (d * n_space + s, (d ^ flip_dp) * n_space + (s ^ flip_space))
        for d in range(lax.axis_size("dp"))
        for s in range(n_space)
    ]
    return lax.ppermute(block, ("dp", "space"), route)


def swap_totals(block):
    n_dp, n_space = lax.axis_size("dp"), lax.axis_size("space")
    if n_dp != 2 or n_space < 2 or n_space & (n_space - 1):
        return lax.psum(block, ("dp", "space")).astype(F32)
    stride = n_space // 2
    while stride > 1:
        other = swapped(block, 0, stride)
        block = (block.astype(F32) + other.astype(F32)).astype(BF16)
        stride //= 2
    both = swapped(block, 1, 1)
    across = swapped(block, 1, 0)
    beside = swapped(block, 0, 1)
    return (block.astype(F32) + across.astype(F32)) + (beside.astype(F32) + both.astype(F32))


def params(mib):
    return pltpu.CompilerParams(vmem_limit_bytes=mib << 20)


def step(features, out_grad, weight_mean, weight_noise, precision):
    feats = jnp.transpose(features[0, 0], (1, 2, 0, 3))
    grads = jnp.transpose(out_grad[0, 0], (1, 2, 0, 3))
    xd, ys, cin, zs = feats.shape
    ni, nj, cout, half = grads.shape
    flat = (weight_mean.size // LANES, LANES)
    mean = weight_mean.reshape(flat)
    prec = precision.reshape(flat)
    noise = weight_noise.reshape(flat)
    width = pl.cdiv(len(TAPS) * cin, LANES) * LANES

    below = passed_along(feats[xd - 1], "space", 1)
    shape = jax.ShapeDtypeStruct
    act_rest, pre_rest, weights, part, total, col = pl.pallas_call(
        prepare_kernel,
        out_shape=(
            shape((ni - 1, nj, cout, half), BF16),
            shape((ni - 1, cout, nj * half), BF16),
            shape((cout, width), BF16),
            shape((cout, nj * half), F32),
            shape((cout, width), F32),
            shape((width, nj * half), BF16),
        ),
        in_specs=[pl.BlockSpec(memory_space=pltpu.HBM)] * 5,
        scratch_shapes=[
            pltpu.VMEM(feats.shape, BF16),
            pltpu.VMEM(grads.shape, BF16),
            pltpu.VMEM(flat, F32),
            pltpu.VMEM(flat, F32),
            pltpu.VMEM(flat, F32),
            pltpu.VMEM((ni - 1, width, nj * half), BF16),
            pltpu.SemaphoreType.DMA((xd + 4,)),
        ],
        compiler_params=params(24),
        name="prepare",
    )(*[pltpu.with_memory_space_constraint(v, pltpu.HBM) for v in (feats, grads, mean, noise, prec)])
    vmem = pl.BlockSpec(memory_space=pltpu.VMEM)
    act, pack, rim, dw = pl.pallas_call(
        finish_kernel,
        out_shape=(
            shape((ni, nj, cout, half), BF16),
            shape((cout, ni * nj * half + width), BF16),
            shape((cout, nj * half), BF16),
            shape(flat, BF16),
        ),
        in_specs=[vmem] * 7 + [pl.BlockSpec(memory_space=pltpu.HBM)],
        scratch_shapes=[
            pltpu.VMEM((len(TAPS) * cin // 3, nj * half), BF16),
            pltpu.VMEM(grads.shape[1:], BF16),
            pltpu.SemaphoreType.DMA,
        ],
        compiler_params=params(24),
        name="finish",
    )(below, act_rest, pre_rest, weights, part, total, col, grads)
    pack = passed_along(pack, "segment", -1)
    rim = passed_diagonally(rim)
    act_in = passed_along(act, "segment", 1)
    grad_in = pl.pallas_call(
        input_kernel,
        out_shape=shape((xd, ys, cin, zs), BF16),
        scratch_shapes=[
            pltpu.VMEM((8 * cin, 8 * cout), BF16),
            pltpu.VMEM((8 * cout, ni * nj * half), BF16),
        ],
        compiler_params=params(24),
        name="input_grad",
    )(pack, rim)
    act_in = pl.pallas_call(
        copy_kernel,
        out_shape=shape(act_in.shape, BF16),
        compiler_params=params(8),
        name="place",
    )(act_in)

    cell_count = lax.axis_size("dp") * lax.axis_size("space") * ni * nj * half
    inv_root = 1.0 / math.sqrt(cell_count)
    scaled = swap_totals(dw) * inv_root
    prec_next = 0.75 * prec + 0.25 * scaled * scaled
    mean_next = mean - 0.03 * scaled / (prec_next + 0.1)
    return (
        jnp.transpose(act_in, (2, 0, 1, 3))[None, None],
        jnp.transpose(grad_in, (2, 0, 1, 3))[None, None],
        mean_next.reshape(weight_mean.shape),
        prec_next.reshape(precision.shape),
    )


def solution(mesh):
    in_specs = (
        P("dp", "segment", None, "space", None, None),
        P("dp", "segment", None, "space", None, None),
        P("segment", None, None),
        P("segment", None, None),
        P("segment", None, None),
    )
    out_specs = (
        P("dp", "segment", None, "space", None, None),
        P("dp", "segment", None, "space", None, None),
        P("segment", None, None),
        P("segment", None, None),
    )
    return jax.shard_map(step, mesh=mesh, in_specs=in_specs, out_specs=out_specs, check_vma=False)
```

```python
import math

import jax
import jax.numpy as jnp
from jax import lax
from jax.experimental import pallas as pl
from jax.experimental.pallas import tpu as pltpu
from jax.sharding import PartitionSpec as P


LANES = 128
TAPS = tuple((a, b, e) for a in range(3) for b in range(3) for e in range(3))
F32 = jnp.float32
BF16 = jnp.bfloat16


def passed_along(block, steps):
    axes = tuple(steps)
    route = [(0, 0)]
    for axis in axes:
        size = lax.axis_size(axis)
        route = [
            (src * size + i, dst * size + (i + steps[axis]) % size)
            for src, dst in route
            for i in range(size)
        ]
    return lax.ppermute(block, axes, route)


def unless(axis, end):
    last = lax.axis_size(axis) - 1 if end else 0
    return jnp.where(lax.axis_index(axis) == last, 0.0, 1.0)


def matmul(a, b):
    return jnp.dot(a, b, preferred_element_type=F32)


def matmul_nt(a, b):
    return lax.dot_general(a, b, (((1,), (1,)), ((), ())), preferred_element_type=F32)


def iota(shape, dim):
    return lax.broadcasted_iota(jnp.int32, shape, dim)


def as_bf16(mask):
    return jnp.where(mask, 1.0, 0.0).astype(BF16)


def pick_strided(zs):
    half = zs // 2
    z = iota((zs, 3 * half), 0)
    n = iota((zs, 3 * half), 1)
    e = jnp.where(n >= 2 * half, 2, jnp.where(n >= half, 1, 0))
    return as_bf16(z == 2 * (n - e * half) + e - 1)


def spread_strided(zs):
    half = zs // 2
    row = iota((zs, zs), 0)
    z = iota((zs, zs), 1)
    p = jnp.where(row >= half, 1, 0)
    return as_bf16(z == 2 * (row - p * half) + p)


def regroup(cout, groups):
    per = cout // groups
    o = iota((cout, cout), 0)
    m = iota((cout, cout), 1)
    oi = jnp.zeros_like(m)
    for step in range(1, groups):
        oi = oi + jnp.where(m >= step * per, 1, 0)
    return as_bf16(o == (m - oi * per) * groups + oi)


def weight_matrix(noisy, cout, cin):
    groups = LANES // cin
    rows = cout // groups
    lane = iota((rows, LANES), 1)
    blocks = []
    for first in range(0, len(TAPS), groups):
        parts = []
        for oi in range(groups):
            part = jnp.zeros((rows, LANES), F32)
            for t in range(groups):
                if first + t >= len(TAPS):
                    continue
                tap = noisy[(first + t) * rows : (first + t + 1) * rows]
                shift = (t - oi) * cin % LANES
                tap = pltpu.roll(tap, shift, 1) if shift else tap
                keep = (lane >= t * cin) & (lane < (t + 1) * cin)
                part = jnp.where(keep, tap, part)
            parts.append(part)
        blocks.append(jnp.concatenate(parts, axis=0))
    mixed = jnp.concatenate(blocks, axis=1).astype(BF16)
    return matmul(regroup(cout, groups), mixed).astype(BF16)


def weight_rows(total, cout, cin):
    groups = LANES // cin
    rows = cout // groups
    lane = iota((rows, LANES), 1)
    mixed = lax.dot_general(
        regroup(cout, groups),
        total.astype(BF16),
        (((0,), (0,)), ((), ())),
        preferred_element_type=F32,
    )
    out = []
    for tap in range(len(TAPS)):
        t = tap % groups
        start = (tap // groups) * LANES
        row = jnp.zeros((rows, LANES), F32)
        for oi in range(groups):
            part = mixed[oi * rows : (oi + 1) * rows, start : start + LANES]
            shift = (oi - t) * cin % LANES
            part = pltpu.roll(part, shift, 1) if shift else part
            keep = (lane >= oi * cin) & (lane < (oi + 1) * cin)
            row = jnp.where(keep, part, row)
        out.append(row)
    return jnp.concatenate(out, axis=0).astype(BF16)


def activate(preact, grads):
    squash = jax.nn.sigmoid(preact)
    act = (preact * squash).astype(BF16)
    pre = (grads * squash * (1.0 + preact * (1.0 - squash))).astype(BF16)
    return act, pre


def place_plane(picked, x, ys, cin, half, targets):
    for tap, (a, b, e) in enumerate(TAPS):
        i = (x + 1 - a) // 2
        if 2 * i + a - 1 != x or i not in targets:
            continue
        for j in range(ys // 2):
            y = 2 * j + b - 1
            if y < 0:
                block = jnp.zeros((cin, half), BF16)
            else:
                block = picked[y * cin : (y + 1) * cin, e * half : (e + 1) * half]
            targets[i][tap * cin : (tap + 1) * cin, j * half : (j + 1) * half] = block


def prepare_kernel(x_hbm, g_hbm, mean_hbm, noise_hbm, prec_hbm,
                   act_ref, pre_ref, w_ref, part_ref, total_ref, col_ref,
                   x_ref, g_ref, mean_ref, noise_ref, prec_ref, cols_ref, sems):
    xd, ys, cin, zs = x_ref.shape
    ni, nj, cout, half = g_ref.shape
    width = w_ref.shape[1]
    depth = len(TAPS) * cin
    order = [pltpu.make_async_copy(x_hbm.at[x], x_ref.at[x], sems.at[x]) for x in range(xd)]
    pairs = ((mean_hbm, mean_ref), (noise_hbm, noise_ref), (prec_hbm, prec_ref), (g_hbm, g_ref))
    rest = [pltpu.make_async_copy(src, dst, sems.at[xd + n]) for n, (src, dst) in enumerate(pairs)]
    for copy in order + rest:
        copy.start()
    targets = {0: col_ref, **{i: cols_ref.at[i - 1] for i in range(1, ni)}}
    for ref in targets.values():
        ref[depth:, :] = jnp.zeros((width - depth, nj * half), BF16)
    pick = pick_strided(zs)
    for x in range(xd):
        order[x].wait()
        picked = matmul(x_ref[x].reshape(ys * cin, zs), pick).astype(BF16)
        place_plane(picked, x, ys, cin, half, targets)
    for copy in rest:
        copy.wait()
    noisy = mean_ref[...] + noise_ref[...] * lax.rsqrt(2000.0 * (prec_ref[...] + 0.1))
    weights = weight_matrix(noisy, cout, cin)
    w_ref[...] = weights
    total = jnp.zeros((cout, width), F32)
    for i in range(1, ni):
        preact = matmul(weights, cols_ref[i - 1])
        grads = jnp.concatenate([g_ref[i, j] for j in range(nj)], axis=1).astype(F32)
        act, pre = activate(preact, grads)
        for j in range(nj):
            act_ref[i - 1, j] = act[:, j * half : (j + 1) * half]
        pre_ref[i - 1] = pre
        total = total + matmul_nt(pre, cols_ref[i - 1])
    total_ref[...] = total
    first = depth // 3
    part_ref[...] = matmul(weights[:, first:], col_ref[first:, :])


def finish_kernel(halo_ref, act_rest_ref, pre_rest_ref, w_ref, part_ref, total_ref, col_in_ref, g_hbm,
                  act_ref, pack_ref, rim_ref, dw_ref, col_ref, g_ref, sem):
    ys, cin, zs = halo_ref.shape
    ni, nj, cout, half = act_ref.shape
    first = len(TAPS) * cin // 3
    copy = pltpu.make_async_copy(g_hbm.at[0], g_ref, sem)
    copy.start()
    picked = matmul(halo_ref[...].reshape(ys * cin, zs), pick_strided(zs))
    picked = (picked * unless("space", 0)).astype(BF16)
    place_plane(picked, -1, ys, cin, half, {0: col_ref})
    preact = part_ref[...] + matmul(w_ref[:, :first], col_ref[...])
    copy.wait()
    grads = jnp.concatenate([g_ref[j] for j in range(nj)], axis=1).astype(F32)
    act, pre = activate(preact, grads)
    for j in range(nj):
        act_ref[0, j] = act[:, j * half : (j + 1) * half]
    act_ref[1:] = act_rest_ref[...]
    rim_ref[...] = pre
    pack_ref[:, : nj * half] = pre
    for i in range(1, ni):
        pack_ref[:, i * nj * half : (i + 1) * nj * half] = pre_rest_ref[i - 1]
    pack_ref[:, ni * nj * half :] = w_ref[...]
    ours = jnp.concatenate([matmul_nt(pre, col_ref[...]), matmul_nt(pre, col_in_ref[first:, :])], axis=1)
    dw_ref[...] = weight_rows(total_ref[...] + ours, cout, cin)


def parity_taps(parity, shift):
    if parity == 0:
        return 1 if shift == 0 else None
    return 2 if shift == 0 else 0


def input_kernel(pack_ref, rim_ref, act_ref, out_hbm, act_hbm,
                 wt_ref, col_ref, out_ref, act_out_ref, sems):
    xd, ys, cin, zs = out_ref.shape
    act_out_ref[...] = (act_ref[...].astype(F32) * unless("segment", 0)).astype(BF16)
    copies = [pltpu.make_async_copy(act_out_ref, act_hbm, sems.at[xd // 2])]
    copies[0].start()
    cout = pack_ref.shape[0]
    half = zs // 2
    ni, nj = xd // 2, ys // 2
    weights = pack_ref[:, ni * nj * half :].astype(F32) * unless("segment", 1)
    rim = (rim_ref[...].astype(F32) * unless("space", 1)).astype(BF16)
    combos = [(p, q, r) for p in range(2) for q in range(2) for r in range(2)]
    flipped = jnp.transpose(
        jnp.concatenate([weights, jnp.zeros((LANES - cout, weights.shape[1]), F32)], axis=0)
    )
    for row, (px, py, pz) in enumerate(combos):
        for col, (di, dj) in enumerate((u, v) for u in range(2) for v in range(2)):
            pair = jnp.zeros((cin, LANES), F32)
            for dk in range(2):
                found = (parity_taps(px, di), parity_taps(py, dj), parity_taps(pz, dk))
                if None in found:
                    continue
                tap = TAPS.index(found)
                block = flipped[tap * cin : (tap + 1) * cin]
                pair = pair + (pltpu.roll(block, cout, 1) if dk else block)
            wt_ref[row * cin : (row + 1) * cin, col * LANES : (col + 1) * LANES] = pair.astype(BF16)
    last = iota((cout, half), 1) == half - 1
    for i in range(ni + 1):
        for j in range(nj + 1):
            if j == nj:
                here = jnp.zeros((cout, half), BF16)
                ahead = here
            else:
                lane = (i * nj + j) * half
                here = rim[:, j * half : (j + 1) * half] if i == ni else pack_ref[:, lane : lane + half]
                ahead = pltpu.roll(here.astype(F32), half - 1, 1)
                ahead = jnp.where(last, 0.0, ahead).astype(BF16)
            for di in range(2):
                for dj in range(2):
                    if not (0 <= i - di < ni and 0 <= j - dj < nj):
                        continue
                    row = (2 * di + dj) * 2 * cout
                    lane = ((i - di) * nj + j - dj) * half
                    col_ref[row : row + cout, lane : lane + half] = here
                    col_ref[row + cout : row + 2 * cout, lane : lane + half] = ahead
    spread = spread_strided(zs)
    for i in range(ni):
        for j in range(nj):
            lane = (i * nj + j) * half
            cells = matmul(wt_ref[...], col_ref[:, lane : lane + half]).astype(BF16)
            pairs = jnp.concatenate(
                [
                    jnp.concatenate(
                        [cells[(2 * n) * cin : (2 * n + 1) * cin], cells[(2 * n + 1) * cin : (2 * n + 2) * cin]],
                        axis=1,
                    )
                    for n in range(4)
                ],
                axis=0,
            )
            planes = matmul(pairs, spread).astype(BF16)
            for n in range(4):
                out_ref[2 * i + n // 2, 2 * j + n % 2] = planes[n * cin : (n + 1) * cin]
        copies.append(
            pltpu.make_async_copy(out_ref.at[2 * i : 2 * i + 2], out_hbm.at[2 * i : 2 * i + 2], sems.at[i])
        )
        copies[-1].start()
    for copy in copies:
        copy.wait()


def swapped(block, flip_dp, flip_space):
    n_space = lax.axis_size("space")
    route = [
        (d * n_space + s, (d ^ flip_dp) * n_space + (s ^ flip_space))
        for d in range(lax.axis_size("dp"))
        for s in range(n_space)
    ]
    return lax.ppermute(block, ("dp", "space"), route)


def swap_totals(block):
    n_dp, n_space = lax.axis_size("dp"), lax.axis_size("space")
    if n_dp != 2 or n_space < 2 or n_space & (n_space - 1):
        return lax.psum(block, ("dp", "space")).astype(F32)
    stride = n_space // 2
    while stride > 1:
        other = swapped(block, 0, stride)
        block = (block.astype(F32) + other.astype(F32)).astype(BF16)
        stride //= 2
    both = swapped(block, 1, 1)
    across = swapped(block, 1, 0)
    beside = swapped(block, 0, 1)
    return (block.astype(F32) + across.astype(F32)) + (beside.astype(F32) + both.astype(F32))


def params(mib):
    return pltpu.CompilerParams(vmem_limit_bytes=mib << 20)


def step(features, out_grad, weight_mean, weight_noise, precision):
    feats = jnp.transpose(features[0, 0], (1, 2, 0, 3))
    grads = jnp.transpose(out_grad[0, 0], (1, 2, 0, 3))
    xd, ys, cin, zs = feats.shape
    ni, nj, cout, half = grads.shape
    flat = (weight_mean.size // LANES, LANES)
    mean = weight_mean.reshape(flat)
    prec = precision.reshape(flat)
    noise = weight_noise.reshape(flat)
    width = pl.cdiv(len(TAPS) * cin, LANES) * LANES

    below = passed_along(feats[xd - 1], {"space": 1})
    shape = jax.ShapeDtypeStruct
    act_rest, pre_rest, weights, part, total, col = pl.pallas_call(
        prepare_kernel,
        out_shape=(
            shape((ni - 1, nj, cout, half), BF16),
            shape((ni - 1, cout, nj * half), BF16),
            shape((cout, width), BF16),
            shape((cout, nj * half), F32),
            shape((cout, width), F32),
            shape((width, nj * half), BF16),
        ),
        in_specs=[pl.BlockSpec(memory_space=pltpu.HBM)] * 5,
        scratch_shapes=[
            pltpu.VMEM(feats.shape, BF16),
            pltpu.VMEM(grads.shape, BF16),
            pltpu.VMEM(flat, F32),
            pltpu.VMEM(flat, F32),
            pltpu.VMEM(flat, F32),
            pltpu.VMEM((ni - 1, width, nj * half), BF16),
            pltpu.SemaphoreType.DMA((xd + 4,)),
        ],
        compiler_params=params(24),
        name="prepare",
    )(*[pltpu.with_memory_space_constraint(v, pltpu.HBM) for v in (feats, grads, mean, noise, prec)])
    vmem = pl.BlockSpec(memory_space=pltpu.VMEM)
    act, pack, rim, dw = pl.pallas_call(
        finish_kernel,
        out_shape=(
            shape((ni, nj, cout, half), BF16),
            shape((cout, ni * nj * half + width), BF16),
            shape((cout, nj * half), BF16),
            shape(flat, BF16),
        ),
        in_specs=[vmem] * 7 + [pl.BlockSpec(memory_space=pltpu.HBM)],
        scratch_shapes=[
            pltpu.VMEM((len(TAPS) * cin // 3, nj * half), BF16),
            pltpu.VMEM(grads.shape[1:], BF16),
            pltpu.SemaphoreType.DMA,
        ],
        compiler_params=params(24),
        name="finish",
    )(below, act_rest, pre_rest, weights, part, total, col, grads)
    pack = passed_along(pack, {"segment": -1})
    rim = passed_along(rim, {"segment": -1, "space": -1})
    act_in = passed_along(act, {"segment": 1})
    hbm = pl.BlockSpec(memory_space=pltpu.HBM)
    grad_in, act_in = pl.pallas_call(
        input_kernel,
        out_shape=(shape((xd, ys, cin, zs), BF16), shape(act.shape, BF16)),
        in_specs=[vmem] * 3,
        out_specs=(hbm, hbm),
        scratch_shapes=[
            pltpu.VMEM((8 * cin, 8 * cout), BF16),
            pltpu.VMEM((8 * cout, ni * nj * half), BF16),
            pltpu.VMEM((xd, ys, cin, zs), BF16),
            pltpu.VMEM(act.shape, BF16),
            pltpu.SemaphoreType.DMA((ni + 1,)),
        ],
        compiler_params=params(24),
        name="input_grad",
    )(pack, rim, act_in)

    cell_count = lax.axis_size("dp") * lax.axis_size("space") * ni * nj * half
    inv_root = 1.0 / math.sqrt(cell_count)
    scaled = swap_totals(dw) * inv_root
    prec_next = 0.75 * prec + 0.25 * scaled * scaled
    mean_next = mean - 0.03 * scaled / (prec_next + 0.1)
    return (
        jnp.transpose(act_in, (2, 0, 1, 3))[None, None],
        jnp.transpose(grad_in, (2, 0, 1, 3))[None, None],
        mean_next.reshape(weight_mean.shape),
        prec_next.reshape(precision.shape),
    )


def solution(mesh):
    in_specs = (
        P("dp", "segment", None, "space", None, None),
        P("dp", "segment", None, "space", None, None),
        P("segment", None, None),
        P("segment", None, None),
        P("segment", None, None),
    )
    out_specs = (
        P("dp", "segment", None, "space", None, None),
        P("dp", "segment", None, "space", None, None),
        P("segment", None, None),
        P("segment", None, None),
    )
    return jax.shard_map(step, mesh=mesh, in_specs=in_specs, out_specs=out_specs, check_vma=False)
```

```python
import math

import jax
import jax.numpy as jnp
from jax import lax
from jax.experimental import pallas as pl
from jax.experimental.pallas import tpu as pltpu
from jax.sharding import PartitionSpec as P


LANES = 128
TAPS = tuple((a, b, e) for a in (1, 2, 0) for b in range(3) for e in range(3))
STORED = tuple(9 * a + 3 * b + e for a, b, e in TAPS)
F32 = jnp.float32
BF16 = jnp.bfloat16


def passed_along(block, steps):
    axes = tuple(steps)
    route = [(0, 0)]
    for axis in axes:
        size = lax.axis_size(axis)
        route = [
            (src * size + i, dst * size + (i + steps[axis]) % size)
            for src, dst in route
            for i in range(size)
        ]
    return lax.ppermute(block, axes, route)


def unless(axis, end):
    last = lax.axis_size(axis) - 1 if end else 0
    return jnp.where(lax.axis_index(axis) == last, 0.0, 1.0)


def matmul(a, b):
    return jnp.dot(a, b, preferred_element_type=F32)


def matmul_nt(a, b):
    return lax.dot_general(a, b, (((1,), (1,)), ((), ())), preferred_element_type=F32)


def iota(shape, dim):
    return lax.broadcasted_iota(jnp.int32, shape, dim)


def as_bf16(mask):
    return jnp.where(mask, 1.0, 0.0).astype(BF16)


def pick_strided(zs):
    half = zs // 2
    z = iota((zs, 3 * half), 0)
    n = iota((zs, 3 * half), 1)
    e = jnp.where(n >= 2 * half, 2, jnp.where(n >= half, 1, 0))
    return as_bf16(z == 2 * (n - e * half) + e - 1)


def spread_strided(zs):
    half = zs // 2
    row = iota((zs, zs), 0)
    z = iota((zs, zs), 1)
    p = jnp.where(row >= half, 1, 0)
    return as_bf16(z == 2 * (row - p * half) + p)


def regroup(cout, groups, back=False):
    per = cout // groups
    o = iota((cout, cout), 0 if back else 1)
    m = iota((cout, cout), 1 if back else 0)
    oi = jnp.zeros_like(m)
    for step in range(1, groups):
        oi = oi + jnp.where(m >= step * per, 1, 0)
    return as_bf16(o == (m - oi * per) * groups + oi)


def weight_matrix(noisy, cout, cin):
    groups = LANES // cin
    rows = cout // groups
    lane = iota((rows, LANES), 1)
    blocks = []
    for first in range(0, len(TAPS), groups):
        parts = []
        for oi in range(groups):
            part = jnp.zeros((rows, LANES), F32)
            for t in range(groups):
                if first + t >= len(TAPS):
                    continue
                stored = STORED[first + t]
                tap = noisy[stored * rows : (stored + 1) * rows]
                shift = (t - oi) * cin % LANES
                tap = pltpu.roll(tap, shift, 1) if shift else tap
                keep = (lane >= t * cin) & (lane < (t + 1) * cin)
                part = jnp.where(keep, tap, part)
            parts.append(part)
        blocks.append(jnp.concatenate(parts, axis=0))
    return jnp.concatenate(blocks, axis=1).astype(BF16)


def weight_rows(total, cout, cin):
    groups = LANES // cin
    rows = cout // groups
    lane = iota((rows, LANES), 1)
    out = []
    for stored in range(len(TAPS)):
        tap = STORED.index(stored)
        t = tap % groups
        start = (tap // groups) * LANES
        row = jnp.zeros((rows, LANES), F32)
        for oi in range(groups):
            part = total[oi * rows : (oi + 1) * rows, start : start + LANES]
            shift = (oi - t) * cin % LANES
            part = pltpu.roll(part, shift, 1) if shift else part
            keep = (lane >= oi * cin) & (lane < (oi + 1) * cin)
            row = jnp.where(keep, part, row)
        out.append(row)
    return jnp.concatenate(out, axis=0).astype(BF16)


def activate(preact, grads):
    squash = jax.nn.sigmoid(preact)
    act = (preact * squash).astype(BF16)
    pre = (grads * squash * (1.0 + preact * (1.0 - squash))).astype(BF16)
    return act, pre


def place_plane(picked, x, ys, cin, half, targets, first=0):
    for tap, (a, b, e) in enumerate(TAPS):
        i = (x + 1 - a) // 2
        if 2 * i + a - 1 != x or i not in targets:
            continue
        for j in range(ys // 2):
            y = 2 * j + b - 1
            if y < 0:
                block = jnp.zeros((cin, half), BF16)
            else:
                block = picked[y * cin : (y + 1) * cin, e * half : (e + 1) * half]
            row = tap * cin - first
            targets[i][row : row + cin, j * half : (j + 1) * half] = block


def plane_kernel(x_hbm, out_ref, sem):
    last = lax.axis_index("space") == lax.axis_size("space") - 1

    @pl.when(last)
    def _():
        out_ref[...] = jnp.zeros(out_ref.shape, out_ref.dtype)

    @pl.when(jnp.logical_not(last))
    def _():
        copy = pltpu.make_async_copy(x_hbm.at[x_hbm.shape[0] - 1], out_ref, sem)
        copy.start()
        copy.wait()


def tail_rows(cin):
    return 2 * len(TAPS) * cin // 3 // LANES * LANES


def prepare_kernel(x_hbm, g_hbm, mean_hbm, noise_hbm, prec_hbm,
                   act_ref, pre_ref, w_ref, part_ref, total_ref, col_ref, pick_ref, g0_ref,
                   x_ref, g_ref, mean_ref, noise_ref, prec_ref, cols_ref, sems):
    xd, ys, cin, zs = x_ref.shape
    ni, nj, cout, half = g_ref.shape
    width = w_ref.shape[1]
    depth = len(TAPS) * cin
    order = [pltpu.make_async_copy(x_hbm.at[x], x_ref.at[x], sems.at[x]) for x in range(xd)]
    pairs = ((mean_hbm, mean_ref), (noise_hbm, noise_ref), (prec_hbm, prec_ref), (g_hbm, g_ref))
    rest = [pltpu.make_async_copy(src, dst, sems.at[xd + n]) for n, (src, dst) in enumerate(pairs)]
    for copy in order + rest:
        copy.start()
    targets = {0: col_ref, **{i: cols_ref.at[i - 1] for i in range(1, ni)}}
    for ref in targets.values():
        ref[depth:, :] = jnp.zeros((width - depth, nj * half), BF16)
    pick = pick_strided(zs)
    pick_ref[...] = pick
    there, back = regroup(cout, LANES // cin), regroup(cout, LANES // cin, True)
    for x in range(0, xd, 2):
        order[x].wait()
        order[x + 1].wait()
        picked = matmul(x_ref[x : x + 2].reshape(2 * ys * cin, zs), pick).astype(BF16)
        place_plane(picked[: ys * cin], x, ys, cin, half, targets)
        place_plane(picked[ys * cin :], x + 1, ys, cin, half, targets)
    for copy in rest:
        copy.wait()
    noisy = mean_ref[...] + noise_ref[...] * lax.rsqrt(2000.0 * (prec_ref[...] + 0.1))
    weights = weight_matrix(noisy, cout, cin)
    w_ref[...] = weights
    total = jnp.zeros((cout, width), F32)
    grads = [matmul(there, jnp.concatenate([g_ref[i, j] for j in range(nj)], axis=1)) for i in range(ni)]
    g0_ref[...] = grads[0]
    for i in range(1, ni):
        preact = matmul(weights, cols_ref[i - 1])
        act, pre = activate(preact, grads[i])
        act = matmul(back, act).astype(BF16)
        for j in range(nj):
            act_ref[i - 1, j] = act[:, j * half : (j + 1) * half]
        pre_ref[i - 1] = pre
        total = total + matmul_nt(pre, cols_ref[i - 1])
    total_ref[...] = total
    tail = tail_rows(cin)
    part_ref[...] = matmul(weights[:, :tail], col_ref[:tail, :])


def finish_kernel(halo_ref, act_rest_ref, pre_rest_ref, w_ref, part_ref, total_ref, col_in_ref, pick_ref, g0_ref,
                  act_ref, pack_ref, rim_ref, dw_ref, col_ref):
    ys, cin, zs = halo_ref.shape
    ni, nj, cout, half = act_ref.shape
    width = w_ref.shape[1]
    depth = len(TAPS) * cin
    tail = tail_rows(cin)
    kept = 2 * depth // 3
    picked = matmul(halo_ref[...].reshape(ys * cin, zs), pick_ref[...]).astype(BF16)
    col_ref[: kept - tail, :] = col_in_ref[tail:kept, :]
    col_ref[depth - tail :, :] = jnp.zeros((width - depth, nj * half), BF16)
    place_plane(picked, -1, ys, cin, half, {0: col_ref}, tail)
    preact = part_ref[...] + matmul(w_ref[:, tail:], col_ref[...])
    act, pre = activate(preact, g0_ref[...])
    ours = jnp.concatenate([matmul_nt(pre, col_in_ref[:tail, :]), matmul_nt(pre, col_ref[...])], axis=1)
    dw_ref[...] = weight_rows(total_ref[...] + ours, cout, cin)
    rim_ref[...] = pre
    act = matmul(regroup(cout, LANES // cin, True), act).astype(BF16)
    for j in range(nj):
        act_ref[0, j] = act[:, j * half : (j + 1) * half]
    act_ref[1:] = act_rest_ref[...]
    pack_ref[:, : nj * half] = pre
    for i in range(1, ni):
        pack_ref[:, i * nj * half : (i + 1) * nj * half] = pre_rest_ref[i - 1]
    pack_ref[:, ni * nj * half :] = w_ref[...]


def parity_taps(parity, shift):
    if parity == 0:
        return 1 if shift == 0 else None
    return 2 if shift == 0 else 0


def input_kernel(pack_ref, rim_ref, act_ref, out_hbm, act_hbm,
                 wt_ref, col_ref, out_ref, act_out_ref, sems):
    xd, ys, cin, zs = out_ref.shape
    act_out_ref[...] = (act_ref[...].astype(F32) * unless("segment", 0)).astype(BF16)
    copies = [pltpu.make_async_copy(act_out_ref, act_hbm, sems.at[xd // 2])]
    copies[0].start()
    cout = pack_ref.shape[0]
    half = zs // 2
    ni, nj = xd // 2, ys // 2
    weights = pack_ref[:, ni * nj * half :].astype(F32) * unless("segment", 1)
    rim = (rim_ref[...].astype(F32) * unless("space", 1)).astype(BF16)
    combos = [(p, q, r) for p in range(2) for q in range(2) for r in range(2)]
    flipped = jnp.transpose(
        jnp.concatenate([weights, jnp.zeros((LANES - cout, weights.shape[1]), F32)], axis=0)
    )
    for row, (px, py, pz) in enumerate(combos):
        for col, (di, dj) in enumerate((u, v) for u in range(2) for v in range(2)):
            pair = jnp.zeros((cin, LANES), F32)
            for dk in range(2):
                found = (parity_taps(px, di), parity_taps(py, dj), parity_taps(pz, dk))
                if None in found:
                    continue
                tap = TAPS.index(found)
                block = flipped[tap * cin : (tap + 1) * cin]
                pair = pair + (pltpu.roll(block, cout, 1) if dk else block)
            wt_ref[row * cin : (row + 1) * cin, col * LANES : (col + 1) * LANES] = pair.astype(BF16)
    last = iota((cout, half), 1) == half - 1
    for i in range(ni + 1):
        for j in range(nj + 1):
            if j == nj:
                here = jnp.zeros((cout, half), BF16)
                ahead = here
            else:
                lane = (i * nj + j) * half
                here = rim[:, j * half : (j + 1) * half] if i == ni else pack_ref[:, lane : lane + half]
                ahead = pltpu.roll(here.astype(F32), half - 1, 1)
                ahead = jnp.where(last, 0.0, ahead).astype(BF16)
            for di in range(2):
                for dj in range(2):
                    if not (0 <= i - di < ni and 0 <= j - dj < nj):
                        continue
                    row = (2 * di + dj) * 2 * cout
                    lane = ((i - di) * nj + j - dj) * half
                    col_ref[row : row + cout, lane : lane + half] = here
                    col_ref[row + cout : row + 2 * cout, lane : lane + half] = ahead
    spread = spread_strided(zs)
    for i in range(ni):
        for j in range(nj):
            lane = (i * nj + j) * half
            cells = matmul(wt_ref[...], col_ref[:, lane : lane + half]).astype(BF16)
            pairs = jnp.concatenate(
                [
                    jnp.concatenate(
                        [cells[(2 * n) * cin : (2 * n + 1) * cin], cells[(2 * n + 1) * cin : (2 * n + 2) * cin]],
                        axis=1,
                    )
                    for n in range(4)
                ],
                axis=0,
            )
            planes = matmul(pairs, spread).astype(BF16)
            for n in range(4):
                out_ref[2 * i + n // 2, 2 * j + n % 2] = planes[n * cin : (n + 1) * cin]
        copies.append(
            pltpu.make_async_copy(out_ref.at[2 * i : 2 * i + 2], out_hbm.at[2 * i : 2 * i + 2], sems.at[i])
        )
        copies[-1].start()
    for copy in copies:
        copy.wait()


def swapped(block, flip_dp, flip_space):
    n_space = lax.axis_size("space")
    route = [
        (d * n_space + s, (d ^ flip_dp) * n_space + (s ^ flip_space))
        for d in range(lax.axis_size("dp"))
        for s in range(n_space)
    ]
    return lax.ppermute(block, ("dp", "space"), route)


def swap_totals(block):
    n_dp, n_space = lax.axis_size("dp"), lax.axis_size("space")
    if n_dp != 2 or n_space < 2 or n_space & (n_space - 1):
        return lax.psum(block, ("dp", "space")).astype(F32)
    stride = n_space // 2
    while stride > 1:
        other = swapped(block, 0, 2 * stride - 1)
        block = (block.astype(F32) + other.astype(F32)).astype(BF16)
        stride //= 2
    both = swapped(block, 1, 1)
    across = swapped(block, 1, 0)
    beside = swapped(block, 0, 1)
    return (block.astype(F32) + across.astype(F32)) + (beside.astype(F32) + both.astype(F32))


def params(mib):
    return pltpu.CompilerParams(vmem_limit_bytes=mib << 20)


def step(features, out_grad, weight_mean, weight_noise, precision):
    feats = jnp.transpose(features[0, 0], (1, 2, 0, 3))
    grads = jnp.transpose(out_grad[0, 0], (1, 2, 0, 3))
    xd, ys, cin, zs = feats.shape
    ni, nj, cout, half = grads.shape
    flat = (weight_mean.size // LANES, LANES)
    mean = weight_mean.reshape(flat)
    prec = precision.reshape(flat)
    noise = weight_noise.reshape(flat)
    width = pl.cdiv(len(TAPS) * cin, LANES) * LANES

    plane = pl.pallas_call(
        plane_kernel,
        out_shape=jax.ShapeDtypeStruct(feats.shape[1:], BF16),
        in_specs=[pl.BlockSpec(memory_space=pltpu.HBM)],
        out_specs=pl.BlockSpec(memory_space=pltpu.VMEM),
        scratch_shapes=[pltpu.SemaphoreType.DMA],
        compiler_params=params(8),
        name="plane",
    )(pltpu.with_memory_space_constraint(feats, pltpu.HBM))
    below = passed_along(plane, {"space": 1})
    shape = jax.ShapeDtypeStruct
    act_rest, pre_rest, weights, part, total, col, pick, grads0 = pl.pallas_call(
        prepare_kernel,
        out_shape=(
            shape((ni - 1, nj, cout, half), BF16),
            shape((ni - 1, cout, nj * half), BF16),
            shape((cout, width), BF16),
            shape((cout, nj * half), F32),
            shape((cout, width), F32),
            shape((width, nj * half), BF16),
            shape((zs, 3 * half), BF16),
            shape((cout, nj * half), F32),
        ),
        in_specs=[pl.BlockSpec(memory_space=pltpu.HBM)] * 5,
        scratch_shapes=[
            pltpu.VMEM(feats.shape, BF16),
            pltpu.VMEM(grads.shape, BF16),
            pltpu.VMEM(flat, F32),
            pltpu.VMEM(flat, F32),
            pltpu.VMEM(flat, F32),
            pltpu.VMEM((ni - 1, width, nj * half), BF16),
            pltpu.SemaphoreType.DMA((xd + 4,)),
        ],
        compiler_params=params(24),
        name="prepare",
    )(*[pltpu.with_memory_space_constraint(v, pltpu.HBM) for v in (feats, grads, mean, noise, prec)])
    vmem = pl.BlockSpec(memory_space=pltpu.VMEM)
    act, pack, rim, dw = pl.pallas_call(
        finish_kernel,
        out_shape=(
            shape((ni, nj, cout, half), BF16),
            shape((cout, ni * nj * half + width), BF16),
            shape((cout, nj * half), BF16),
            shape(flat, BF16),
        ),
        in_specs=[vmem] * 9,
        scratch_shapes=[pltpu.VMEM((width - tail_rows(cin), nj * half), BF16)],
        compiler_params=params(24),
        name="finish",
    )(below, act_rest, pre_rest, weights, part, total, col, pick, grads0)
    pack = passed_along(pack, {"segment": -1})
    rim = passed_along(rim, {"segment": -1, "space": -1})
    act_in = passed_along(act, {"segment": 1})
    hbm = pl.BlockSpec(memory_space=pltpu.HBM)
    grad_in, act_in = pl.pallas_call(
        input_kernel,
        out_shape=(shape((xd, ys, cin, zs), BF16), shape(act.shape, BF16)),
        in_specs=[vmem] * 3,
        out_specs=(hbm, hbm),
        scratch_shapes=[
            pltpu.VMEM((8 * cin, 8 * cout), BF16),
            pltpu.VMEM((8 * cout, ni * nj * half), BF16),
            pltpu.VMEM((xd, ys, cin, zs), BF16),
            pltpu.VMEM(act.shape, BF16),
            pltpu.SemaphoreType.DMA((ni + 1,)),
        ],
        compiler_params=params(24),
        name="input_grad",
    )(pack, rim, act_in)

    cell_count = lax.axis_size("dp") * lax.axis_size("space") * ni * nj * half
    inv_root = 1.0 / math.sqrt(cell_count)
    scaled = swap_totals(dw) * inv_root
    prec_next = 0.75 * prec + 0.25 * scaled * scaled
    mean_next = mean - 0.03 * scaled / (prec_next + 0.1)
    return (
        jnp.transpose(act_in, (2, 0, 1, 3))[None, None],
        jnp.transpose(grad_in, (2, 0, 1, 3))[None, None],
        mean_next.reshape(weight_mean.shape),
        prec_next.reshape(precision.shape),
    )


def solution(mesh):
    in_specs = (
        P("dp", "segment", None, "space", None, None),
        P("dp", "segment", None, "space", None, None),
        P("segment", None, None),
        P("segment", None, None),
        P("segment", None, None),
    )
    out_specs = (
        P("dp", "segment", None, "space", None, None),
        P("dp", "segment", None, "space", None, None),
        P("segment", None, None),
        P("segment", None, None),
    )
    return jax.shard_map(step, mesh=mesh, in_specs=in_specs, out_specs=out_specs, check_vma=False)
```

```python
import math

import jax
import jax.numpy as jnp
from jax import lax
from jax.experimental import pallas as pl
from jax.experimental.pallas import tpu as pltpu
from jax.sharding import PartitionSpec as P


LANES = 128
TAPS = tuple((a, b, e) for a in (1, 2, 0) for b in range(3) for e in range(3))
STORED = tuple(9 * a + 3 * b + e for a, b, e in TAPS)
F32 = jnp.float32
BF16 = jnp.bfloat16


def passed_along(block, steps):
    axes = tuple(steps)
    route = [(0, 0)]
    for axis in axes:
        size = lax.axis_size(axis)
        route = [
            (src * size + i, dst * size + (i + steps[axis]) % size)
            for src, dst in route
            for i in range(size)
        ]
    return lax.ppermute(block, axes, route)


def unless(axis, end):
    last = lax.axis_size(axis) - 1 if end else 0
    return jnp.where(lax.axis_index(axis) == last, 0.0, 1.0)


def matmul(a, b):
    return jnp.dot(a, b, preferred_element_type=F32)


def matmul_nt(a, b):
    return lax.dot_general(a, b, (((1,), (1,)), ((), ())), preferred_element_type=F32)


def iota(shape, dim):
    return lax.broadcasted_iota(jnp.int32, shape, dim)


def as_bf16(mask):
    return jnp.where(mask, 1.0, 0.0).astype(BF16)


def pick_strided(zs):
    half = zs // 2
    z = iota((zs, 3 * half), 0)
    n = iota((zs, 3 * half), 1)
    e = jnp.where(n >= 2 * half, 2, jnp.where(n >= half, 1, 0))
    return as_bf16(z == 2 * (n - e * half) + e - 1)


def spread_strided(zs):
    half = zs // 2
    row = iota((zs, zs), 0)
    z = iota((zs, zs), 1)
    p = jnp.where(row >= half, 1, 0)
    return as_bf16(z == 2 * (row - p * half) + p)


def regroup(cout, groups, back=False):
    per = cout // groups
    o = iota((cout, cout), 0 if back else 1)
    m = iota((cout, cout), 1 if back else 0)
    oi = jnp.zeros_like(m)
    for step in range(1, groups):
        oi = oi + jnp.where(m >= step * per, 1, 0)
    return as_bf16(o == (m - oi * per) * groups + oi)


def weight_matrix(noisy, cout, cin):
    groups = LANES // cin
    rows = cout // groups
    lane = iota((rows, LANES), 1)
    blocks = []
    for first in range(0, len(TAPS), groups):
        parts = []
        for oi in range(groups):
            part = jnp.zeros((rows, LANES), F32)
            for t in range(groups):
                if first + t >= len(TAPS):
                    continue
                stored = STORED[first + t]
                tap = noisy[stored * rows : (stored + 1) * rows]
                shift = (t - oi) * cin % LANES
                tap = pltpu.roll(tap, shift, 1) if shift else tap
                keep = (lane >= t * cin) & (lane < (t + 1) * cin)
                part = jnp.where(keep, tap, part)
            parts.append(part)
        blocks.append(jnp.concatenate(parts, axis=0))
    return jnp.concatenate(blocks, axis=1).astype(BF16)


def weight_rows(total, cout, cin):
    groups = LANES // cin
    rows = cout // groups
    lane = iota((rows, LANES), 1)
    out = []
    for stored in range(len(TAPS)):
        tap = STORED.index(stored)
        t = tap % groups
        start = (tap // groups) * LANES
        row = jnp.zeros((rows, LANES), F32)
        for oi in range(groups):
            part = total[oi * rows : (oi + 1) * rows, start : start + LANES]
            shift = (oi - t) * cin % LANES
            part = pltpu.roll(part, shift, 1) if shift else part
            keep = (lane >= oi * cin) & (lane < (oi + 1) * cin)
            row = jnp.where(keep, part, row)
        out.append(row)
    return jnp.concatenate(out, axis=0).astype(BF16)


def activate(preact, grads):
    squash = jax.nn.sigmoid(preact)
    act = (preact * squash).astype(BF16)
    pre = (grads * squash * (1.0 + preact * (1.0 - squash))).astype(BF16)
    return act, pre


def place_plane(picked, x, ys, cin, half, targets, first=0):
    for tap, (a, b, e) in enumerate(TAPS):
        i = (x + 1 - a) // 2
        if 2 * i + a - 1 != x or i not in targets:
            continue
        for j in range(ys // 2):
            y = 2 * j + b - 1
            if y < 0:
                block = jnp.zeros((cin, half), BF16)
            else:
                block = picked[y * cin : (y + 1) * cin, e * half : (e + 1) * half]
            row = tap * cin - first
            targets[i][row : row + cin, j * half : (j + 1) * half] = block


def plane_kernel(x_hbm, out_ref, sem):
    last = lax.axis_index("space") == lax.axis_size("space") - 1

    @pl.when(last)
    def _():
        out_ref[...] = jnp.zeros(out_ref.shape, out_ref.dtype)

    @pl.when(jnp.logical_not(last))
    def _():
        copy = pltpu.make_async_copy(x_hbm.at[x_hbm.shape[0] - 1], out_ref, sem)
        copy.start()
        copy.wait()


def tail_rows(cin):
    return 2 * len(TAPS) * cin // 3 // LANES * LANES


def prepare_kernel(x_hbm, g_hbm, mean_hbm, noise_hbm, prec_hbm,
                   act_ref, pre_ref, w_ref, part_ref, total_ref, col_ref, pick_ref, g0_ref,
                   x_ref, g_ref, mean_ref, noise_ref, prec_ref, cols_ref, sems):
    xd, ys, cin, zs = x_ref.shape
    ni, nj, cout, half = g_ref.shape
    width = w_ref.shape[1]
    depth = len(TAPS) * cin
    order = [pltpu.make_async_copy(x_hbm.at[x], x_ref.at[x], sems.at[x]) for x in range(xd)]
    pairs = ((mean_hbm, mean_ref), (noise_hbm, noise_ref), (prec_hbm, prec_ref), (g_hbm, g_ref))
    rest = [pltpu.make_async_copy(src, dst, sems.at[xd + n]) for n, (src, dst) in enumerate(pairs)]
    for copy in order + rest:
        copy.start()
    targets = {0: col_ref, **{i: cols_ref.at[i - 1] for i in range(1, ni)}}
    for ref in targets.values():
        ref[depth:, :] = jnp.zeros((width - depth, nj * half), BF16)
    pick = pick_strided(zs)
    pick_ref[...] = pick
    there, back = regroup(cout, LANES // cin), regroup(cout, LANES // cin, True)
    for x in range(xd):
        order[x].wait()
    every = matmul(x_ref[...].reshape(xd * ys * cin, zs), pick).astype(BF16)
    for x in range(xd):
        place_plane(every[x * ys * cin : (x + 1) * ys * cin], x, ys, cin, half, targets)
    for copy in rest:
        copy.wait()
    noisy = mean_ref[...] + noise_ref[...] * lax.rsqrt(2000.0 * (prec_ref[...] + 0.1))
    weights = weight_matrix(noisy, cout, cin)
    w_ref[...] = weights
    total = jnp.zeros((cout, width), F32)
    grads = [matmul(there, jnp.concatenate([g_ref[i, j] for j in range(nj)], axis=1)) for i in range(ni)]
    g0_ref[...] = grads[0]
    for i in range(1, ni):
        preact = matmul(weights, cols_ref[i - 1])
        act, pre = activate(preact, grads[i])
        act = matmul(back, act).astype(BF16)
        for j in range(nj):
            act_ref[i - 1, j] = act[:, j * half : (j + 1) * half]
        pre_ref[i - 1] = pre
        total = total + matmul_nt(pre, cols_ref[i - 1])
    total_ref[...] = total
    tail = tail_rows(cin)
    part_ref[...] = matmul(weights[:, :tail], col_ref[:tail, :])


def finish_kernel(halo_ref, act_rest_ref, pre_rest_ref, w_ref, part_ref, total_ref, col_in_ref, pick_ref, g0_ref,
                  act_ref, pack_ref, rim_ref, dw_ref, col_ref):
    ys, cin, zs = halo_ref.shape
    ni, nj, cout, half = act_ref.shape
    width = w_ref.shape[1]
    depth = len(TAPS) * cin
    tail = tail_rows(cin)
    kept = 2 * depth // 3
    picked = matmul(halo_ref[...].reshape(ys * cin, zs), pick_ref[...]).astype(BF16)
    col_ref[: kept - tail, :] = col_in_ref[tail:kept, :]
    col_ref[depth - tail :, :] = jnp.zeros((width - depth, nj * half), BF16)
    place_plane(picked, -1, ys, cin, half, {0: col_ref}, tail)
    preact = part_ref[...] + matmul(w_ref[:, tail:], col_ref[...])
    act, pre = activate(preact, g0_ref[...])
    ours = jnp.concatenate([matmul_nt(pre, col_in_ref[:tail, :]), matmul_nt(pre, col_ref[...])], axis=1)
    dw_ref[...] = weight_rows(total_ref[...] + ours, cout, cin)
    rim_ref[...] = pre
    act = matmul(regroup(cout, LANES // cin, True), act).astype(BF16)
    for j in range(nj):
        act_ref[0, j] = act[:, j * half : (j + 1) * half]
    act_ref[1:] = act_rest_ref[...]
    pack_ref[:, : nj * half] = pre
    for i in range(1, ni):
        pack_ref[:, i * nj * half : (i + 1) * nj * half] = pre_rest_ref[i - 1]
    pack_ref[:, ni * nj * half :] = w_ref[...]


def parity_taps(parity, shift):
    if parity == 0:
        return 1 if shift == 0 else None
    return 2 if shift == 0 else 0


def input_kernel(pack_ref, rim_ref, act_ref, out_hbm, act_hbm,
                 wt_ref, col_ref, out_ref, act_out_ref, sems):
    xd, ys, cin, zs = out_ref.shape
    act_out_ref[...] = (act_ref[...].astype(F32) * unless("segment", 0)).astype(BF16)
    copies = [pltpu.make_async_copy(act_out_ref, act_hbm, sems.at[xd // 2])]
    copies[0].start()
    cout = pack_ref.shape[0]
    half = zs // 2
    ni, nj = xd // 2, ys // 2
    weights = pack_ref[:, ni * nj * half :].astype(F32) * unless("segment", 1)
    rim = (rim_ref[...].astype(F32) * unless("space", 1)).astype(BF16)
    combos = [(p, q, r) for p in range(2) for q in range(2) for r in range(2)]
    flipped = jnp.transpose(
        jnp.concatenate([weights, jnp.zeros((LANES - cout, weights.shape[1]), F32)], axis=0)
    )
    for row, (px, py, pz) in enumerate(combos):
        for col, (di, dj) in enumerate((u, v) for u in range(2) for v in range(2)):
            pair = jnp.zeros((cin, LANES), F32)
            for dk in range(2):
                found = (parity_taps(px, di), parity_taps(py, dj), parity_taps(pz, dk))
                if None in found:
                    continue
                tap = TAPS.index(found)
                block = flipped[tap * cin : (tap + 1) * cin]
                pair = pair + (pltpu.roll(block, cout, 1) if dk else block)
            wt_ref[row * cin : (row + 1) * cin, col * LANES : (col + 1) * LANES] = pair.astype(BF16)
    last = iota((cout, half), 1) == half - 1
    for i in range(ni + 1):
        for j in range(nj + 1):
            if j == nj:
                here = jnp.zeros((cout, half), BF16)
                ahead = here
            else:
                lane = (i * nj + j) * half
                here = rim[:, j * half : (j + 1) * half] if i == ni else pack_ref[:, lane : lane + half]
                ahead = pltpu.roll(here.astype(F32), half - 1, 1)
                ahead = jnp.where(last, 0.0, ahead).astype(BF16)
            for di in range(2):
                for dj in range(2):
                    if not (0 <= i - di < ni and 0 <= j - dj < nj):
                        continue
                    row = (2 * di + dj) * 2 * cout
                    lane = ((i - di) * nj + j - dj) * half
                    col_ref[row : row + cout, lane : lane + half] = here
                    col_ref[row + cout : row + 2 * cout, lane : lane + half] = ahead
    spread = spread_strided(zs)
    for i in range(ni):
        for j in range(nj):
            lane = (i * nj + j) * half
            cells = matmul(wt_ref[...], col_ref[:, lane : lane + half]).astype(BF16)
            pairs = jnp.concatenate(
                [
                    jnp.concatenate(
                        [cells[(2 * n) * cin : (2 * n + 1) * cin], cells[(2 * n + 1) * cin : (2 * n + 2) * cin]],
                        axis=1,
                    )
                    for n in range(4)
                ],
                axis=0,
            )
            planes = matmul(pairs, spread).astype(BF16)
            for n in range(4):
                out_ref[2 * i + n // 2, 2 * j + n % 2] = planes[n * cin : (n + 1) * cin]
        copies.append(
            pltpu.make_async_copy(out_ref.at[2 * i : 2 * i + 2], out_hbm.at[2 * i : 2 * i + 2], sems.at[i])
        )
        copies[-1].start()
    for copy in copies:
        copy.wait()


def swapped(block, flip_dp, flip_space):
    n_space = lax.axis_size("space")
    route = [
        (d * n_space + s, (d ^ flip_dp) * n_space + (s ^ flip_space))
        for d in range(lax.axis_size("dp"))
        for s in range(n_space)
    ]
    return lax.ppermute(block, ("dp", "space"), route)


def swap_totals(block):
    n_dp, n_space = lax.axis_size("dp"), lax.axis_size("space")
    if n_dp != 2 or n_space < 2 or n_space & (n_space - 1):
        return lax.psum(block, ("dp", "space")).astype(F32)
    stride = n_space // 2
    while stride > 1:
        other = swapped(block, 0, 2 * stride - 1)
        block = (block.astype(F32) + other.astype(F32)).astype(BF16)
        stride //= 2
    both = swapped(block, 1, 1)
    across = swapped(block, 1, 0)
    beside = swapped(block, 0, 1)
    return (block.astype(F32) + across.astype(F32)) + (beside.astype(F32) + both.astype(F32))


def params(mib):
    return pltpu.CompilerParams(vmem_limit_bytes=mib << 20)


def step(features, out_grad, weight_mean, weight_noise, precision):
    feats = jnp.transpose(features[0, 0], (1, 2, 0, 3))
    grads = jnp.transpose(out_grad[0, 0], (1, 2, 0, 3))
    xd, ys, cin, zs = feats.shape
    ni, nj, cout, half = grads.shape
    flat = (weight_mean.size // LANES, LANES)
    mean = weight_mean.reshape(flat)
    prec = precision.reshape(flat)
    noise = weight_noise.reshape(flat)
    width = pl.cdiv(len(TAPS) * cin, LANES) * LANES

    plane = pl.pallas_call(
        plane_kernel,
        out_shape=jax.ShapeDtypeStruct(feats.shape[1:], BF16),
        in_specs=[pl.BlockSpec(memory_space=pltpu.HBM)],
        out_specs=pl.BlockSpec(memory_space=pltpu.VMEM),
        scratch_shapes=[pltpu.SemaphoreType.DMA],
        compiler_params=params(8),
        name="plane",
    )(pltpu.with_memory_space_constraint(feats, pltpu.HBM))
    below = passed_along(plane, {"space": 1})
    shape = jax.ShapeDtypeStruct
    act_rest, pre_rest, weights, part, total, col, pick, grads0 = pl.pallas_call(
        prepare_kernel,
        out_shape=(
            shape((ni - 1, nj, cout, half), BF16),
            shape((ni - 1, cout, nj * half), BF16),
            shape((cout, width), BF16),
            shape((cout, nj * half), F32),
            shape((cout, width), F32),
            shape((width, nj * half), BF16),
            shape((zs, 3 * half), BF16),
            shape((cout, nj * half), F32),
        ),
        in_specs=[pl.BlockSpec(memory_space=pltpu.HBM)] * 5,
        scratch_shapes=[
            pltpu.VMEM(feats.shape, BF16),
            pltpu.VMEM(grads.shape, BF16),
            pltpu.VMEM(flat, F32),
            pltpu.VMEM(flat, F32),
            pltpu.VMEM(flat, F32),
            pltpu.VMEM((ni - 1, width, nj * half), BF16),
            pltpu.SemaphoreType.DMA((xd + 4,)),
        ],
        compiler_params=params(24),
        name="prepare",
    )(*[pltpu.with_memory_space_constraint(v, pltpu.HBM) for v in (feats, grads, mean, noise, prec)])
    vmem = pl.BlockSpec(memory_space=pltpu.VMEM)
    act, pack, rim, dw = pl.pallas_call(
        finish_kernel,
        out_shape=(
            shape((ni, nj, cout, half), BF16),
            shape((cout, ni * nj * half + width), BF16),
            shape((cout, nj * half), BF16),
            shape(flat, BF16),
        ),
        in_specs=[vmem] * 9,
        scratch_shapes=[pltpu.VMEM((width - tail_rows(cin), nj * half), BF16)],
        compiler_params=params(24),
        name="finish",
    )(below, act_rest, pre_rest, weights, part, total, col, pick, grads0)
    pack = passed_along(pack, {"segment": -1})
    rim = passed_along(rim, {"segment": -1, "space": -1})
    act_in = passed_along(act, {"segment": 1})
    hbm = pl.BlockSpec(memory_space=pltpu.HBM)
    grad_in, act_in = pl.pallas_call(
        input_kernel,
        out_shape=(shape((xd, ys, cin, zs), BF16), shape(act.shape, BF16)),
        in_specs=[vmem] * 3,
        out_specs=(hbm, hbm),
        scratch_shapes=[
            pltpu.VMEM((8 * cin, 8 * cout), BF16),
            pltpu.VMEM((8 * cout, ni * nj * half), BF16),
            pltpu.VMEM((xd, ys, cin, zs), BF16),
            pltpu.VMEM(act.shape, BF16),
            pltpu.SemaphoreType.DMA((ni + 1,)),
        ],
        compiler_params=params(24),
        name="input_grad",
    )(pack, rim, act_in)

    cell_count = lax.axis_size("dp") * lax.axis_size("space") * ni * nj * half
    inv_root = 1.0 / math.sqrt(cell_count)
    scaled = swap_totals(dw) * inv_root
    prec_next = 0.75 * prec + 0.25 * scaled * scaled
    mean_next = mean - 0.03 * scaled / (prec_next + 0.1)
    return (
        jnp.transpose(act_in, (2, 0, 1, 3))[None, None],
        jnp.transpose(grad_in, (2, 0, 1, 3))[None, None],
        mean_next.reshape(weight_mean.shape),
        prec_next.reshape(precision.shape),
    )


def solution(mesh):
    in_specs = (
        P("dp", "segment", None, "space", None, None),
        P("dp", "segment", None, "space", None, None),
        P("segment", None, None),
        P("segment", None, None),
        P("segment", None, None),
    )
    out_specs = (
        P("dp", "segment", None, "space", None, None),
        P("dp", "segment", None, "space", None, None),
        P("segment", None, None),
        P("segment", None, None),
    )
    return jax.shard_map(step, mesh=mesh, in_specs=in_specs, out_specs=out_specs, check_vma=False)
```
